32 devices in a mesh: fsdp: 4 (over z), dp: 2 (over y), tensor: 4 (over x, core).
Axes of the slice: x: 2, y: 2, z: 4, core: 2. Of those that a mesh axis runs over, the one named last changes fastest.
Arguments:
- tokens: bfloat16 [2048, 7168], P(('fsdp', 'dp')), may hold values from -6 to 6
- panels: bfloat16 [112, 4, 128, 128], P('tensor', None, 'fsdp'), may hold values from -0.25 to 0.25
- block_rows: int32 [112, 4], P('tensor'), may hold values from 0 to 55, as said below
- low_in: bfloat16 [7168, 512], P('tensor'), may hold values from -0.0625 to 0.0625
- low_out: bfloat16 [112, 4, 128, 128], P('tensor'), may hold values from -0.25 to 0.25
- cotangent: bfloat16 [2048, 14336], P(('fsdp', 'dp'), 'tensor'), may hold values from -0.125 to 0.125
Outputs:
- activated: bfloat16 [2048, 14336], P(('fsdp', 'dp'), 'tensor')
- panel_grad: float32 [112, 4, 128, 128], P('tensor', None, 'fsdp')
The draws below stay inside these ranges and needn't reach their ends.
Inputs may be any that keep to these rules, and one draw needn't show every extreme that they name: `block_rows`: each column block c names 4 distinct row blocks, the first of them c modulo 56.
All inputs are finite; a program needn't handle non-finite values.
Results may differ from the reference program's by a relative error of at most 0.0039.
Values may be sent and summed in bfloat16 or wider, within the bound.
A program may use at most 128 MiB of HBM per device.

```python
import jax
import jax.numpy as jnp
from jax import lax

D = 7168
FF = 14336
BLK = 128
K = 4
R = 512
RB = 56
CB = 112
RBLK = 4
TOKENS = 2048


def draw_block_rows(key, part):
    scores = jax.random.randint(key, (CB, RB), 0, 1 << 20)
    column = lax.broadcasted_iota(jnp.int32, (CB, RB), 0)
    within = lax.broadcasted_iota(jnp.int32, (CB, RB), 1)
    scores = scores * RB + within
    scores = jnp.where(within == column % RB, -1, scores)
    ranking = jnp.argsort(scores, axis=1, stable=True)
    return ranking[:, :K].astype(jnp.int32)


def steps_of(key, shape, cuts, smallest, high):
    def one(axis_at, shards_of):
        heights = jax.random.uniform(jax.random.fold_in(jax.random.fold_in(key, 6), axis_at), (shards_of,), jnp.float32, smallest / len(cuts), high / len(cuts))
        return jnp.repeat(jnp.exp(heights), shape[axis_at] // shards_of).reshape((-1,) + (1,) * (len(shape) - axis_at - 1))

    gain = one(*cuts[0])
    for cut in cuts[1:]:
        gain = gain * one(*cut)
    return gain


def scatter_about(key, extent, width, bound, cuts=(), dtype=jnp.bfloat16):
    loudness = steps_of(key, extent, cuts, -0.22, 0.18) if cuts else 1.0
    drawn = jax.random.normal(key, extent, jnp.float32) * width * loudness
    return jnp.minimum(jnp.maximum(drawn, -bound), bound).astype(dtype)


def setup_inputs(seed: int = 0) -> dict:
    splits = jax.random.split(jax.random.key(seed), 7)
    tokens = scatter_about(splits[0], (TOKENS, D), 1.0, 6.0, ((0, 8),))
    panels = scatter_about(splits[1], (CB, K, BLK, BLK), (K * BLK) ** -0.5, 0.25, ((0, 4), (2, 4)))
    block_rows = draw_block_rows(jax.random.fold_in(splits[6], 71), 0)
    low_in = scatter_about(splits[3], (D, R), D ** -0.5, 0.0625, ((0, 4),))
    low_out = scatter_about(splits[4], (CB, RBLK, BLK, BLK), R ** -0.5, 0.25, ((0, 4),))
    cotangent = scatter_about(splits[5], (TOKENS, FF), TOKENS ** -0.5, 0.125, ((0, 8), (1, 4)))
    return {"tokens": tokens, "panels": panels, "block_rows": block_rows, "low_in": low_in, "low_out": low_out, "cotangent": cotangent}


def activate(values):
    return jax.nn.gelu(values, approximate=True)

def reference(tokens, panels, block_rows, low_in, low_out, cotangent):
    latent = jnp.dot(tokens, low_in, preferred_element_type=jnp.float32).astype(jnp.bfloat16)
    latent_tiles = latent.reshape(TOKENS, RBLK, BLK).astype(jnp.float32)
    tiled_rows = tokens.reshape(TOKENS, RB, BLK)
    slopes_in = jnp.transpose(cotangent.reshape(TOKENS, CB, BLK), (1, 0, 2))

    def one_column(inputs):
        rows_here, panel_here, lowout_here, slope_in = inputs
        picked = jnp.take(tiled_rows, rows_here.astype(jnp.int32), axis=1).astype(jnp.float32)
        low_part = jnp.einsum('tjr,jro->to', latent_tiles, lowout_here.astype(jnp.float32))
        sparse_part = jnp.einsum('tkr,kro->to', picked, panel_here.astype(jnp.float32))
        pre = low_part + sparse_part
        result, pullback = jax.vjp(activate, pre)
        slope = pullback(slope_in.astype(jnp.float32))[0].astype(jnp.bfloat16)
        grad_here = jnp.einsum('tkr,to->kro', picked, slope.astype(jnp.float32))
        return (result.astype(jnp.bfloat16), grad_here)
    outputs, panel_grad = lax.map(one_column, (block_rows, panels, low_out, slopes_in))
    activated = jnp.transpose(outputs, (1, 0, 2)).reshape(TOKENS, FF)
    return (activated, panel_grad)
```

```python
import functools
import math

import jax
import jax.numpy as jnp
from jax import lax
from jax.experimental import pallas as pl
from jax.experimental.pallas import tpu as pltpu
from jax.sharding import PartitionSpec as P

MESH = pl.DeviceIdType.MESH
GELU_SCALE = math.sqrt(2.0 / math.pi)
GELU_CUBIC = 0.044715
AHEAD = 2


def kernel(
    nz, ny, nt, nc,
    tokens_hbm, panels_hbm, rows_ref, low_in_hbm, low_out_hbm, cot_hbm,
    act_ref, grad_ref,
    tok, lin, lout, cot, pan, own, sbuf, rbuf, ysend, yrecv, lpart, lrecv, lat,
    local_sem, tok_sem, ag_send, ag_recv, rs_send, rs_recv, y_send, y_recv,
    l1_send, l1_recv, l2_send, l2_recv,
):
    z, y, t = lax.axis_index("fsdp"), lax.axis_index("dp"), lax.axis_index("tensor")
    cols, per, rows, blk = panels_hbm.shape
    chunks = cols // nc
    f32 = jnp.float32

    in_copies = [
        pltpu.make_async_copy(src, dst, local_sem.at[i])
        for i, (src, dst) in enumerate(
            [(low_in_hbm, lin), (panels_hbm, pan.at[z]), (low_out_hbm, lout), (cot_hbm, cot)]
        )
    ]
    feature_blocks, toks = tok.shape[:2]

    def token_copy(b):
        return pltpu.make_async_copy(
            tokens_hbm.at[:, pl.ds(pl.multiple_of(b * blk, blk), blk)], tok.at[b], tok_sem.at[b])

    def token_start(b, carry):
        token_copy(b).start()
        return carry

    def token_wait(b, carry):
        token_copy(b).wait()
        return carry

    in_copies[0].start()
    lax.fori_loop(0, feature_blocks, token_start, 0)
    for copy in in_copies[1:]:
        copy.start()

    barrier = pltpu.get_barrier_semaphore()

    @pl.when(z > 0)
    def _():
        pl.semaphore_signal(barrier, inc=1, device_id={"fsdp": z - 1}, device_id_type=MESH)

    @pl.when(z < nz - 1)
    def _():
        pl.semaphore_signal(barrier, inc=1, device_id={"fsdp": z + 1}, device_id_type=MESH)

    for i in range(1, nt):
        pl.semaphore_signal(
            barrier, inc=1, device_id={"tensor": lax.rem(t + i, nt)}, device_id_type=MESH)
    for i in range(1, ny):
        pl.semaphore_signal(
            barrier, inc=1, device_id={"dp": lax.rem(y + i, ny)}, device_id_type=MESH)
    neighbours = jnp.where(z > 0, 1, 0) + jnp.where(z < nz - 1, 1, 0)
    pl.semaphore_wait(barrier, nt - 1 + ny - 1 + neighbours)

    def span(j):
        return pl.ds(j * nc, nc)

    def gather_copy(way, shard, j, own_part):
        there = z + 1 if way == 0 else z - 1
        src = panels_hbm.at[span(j)] if own_part else pan.at[shard, span(j)]
        return pltpu.make_async_remote_copy(
            src_ref=src, dst_ref=pan.at[shard, span(j)],
            send_sem=ag_send.at[way, shard, j], recv_sem=ag_recv.at[shard, j],
            device_id={"fsdp": there}, device_id_type=MESH)

    def send_own(j):
        @pl.when(z < nz - 1)
        def _():
            gather_copy(0, z, j, True).start()

        @pl.when(z > 0)
        def _():
            gather_copy(1, z, j, True).start()

    def inside(j):
        return jnp.logical_and(j >= 0, j < chunks)

    def pass_on(h, tau):
        j = tau - (h - 1)
        ok = inside(j)

        @pl.when(jnp.logical_and(ok, z - h >= 0))
        def _():
            gather_copy(0, z - h, j, False).wait_recv()

            @pl.when(z < nz - 1)
            def _():
                gather_copy(0, z - h, j, False).start()

        @pl.when(jnp.logical_and(ok, z + h < nz))
        def _():
            gather_copy(1, z + h, j, False).wait_recv()

            @pl.when(z > 0)
            def _():
                gather_copy(1, z + h, j, False).start()

    for j in range(min(AHEAD, chunks)):
        send_own(j)

    in_copies[0].wait()
    lax.fori_loop(0, feature_blocks, token_wait, 0)
    blocks = lin.shape[0] // blk
    lpart[...] = jnp.dot(
        jnp.concatenate([tok[t * blocks + b] for b in range(blocks)], axis=1), lin[...],
        preferred_element_type=f32,
    ).reshape(lpart.shape)

    def lat_one(i):
        peer = lax.rem(t + i, nt)
        return pltpu.make_async_remote_copy(
            src_ref=lpart.at[peer], dst_ref=lrecv.at[i],
            send_sem=l1_send.at[i], recv_sem=l1_recv.at[i],
            device_id={"tensor": peer}, device_id_type=MESH)

    def lat_two(i, shard):
        peer = lax.rem(t + i, nt)
        return pltpu.make_async_remote_copy(
            src_ref=lat.at[shard], dst_ref=lat.at[shard],
            send_sem=l2_send.at[i], recv_sem=l2_recv.at[i],
            device_id={"tensor": peer}, device_id_type=MESH)

    for i in range(1, nt):
        lat_one(i).start()
    total = lpart[t]
    for i in range(1, nt):
        lat_one(i).wait_recv()
        total = total + lrecv[i]
    lat[t] = total.astype(lat.dtype)
    for i in range(1, nt):
        lat_two(i, t).start()
    for copy in in_copies[1:]:
        copy.wait()
    for i in range(1, nt):
        lat_two(i, lax.rem(t + nt - i, nt)).wait_recv()

    def column(c):
        picked = jnp.concatenate(
            [tok[rows_ref[c, k]] for k in range(per)], axis=1)
        weight = jnp.concatenate(
            [pan[s, c, k] for k in range(per) for s in range(nz)], axis=0)
        latent = lat[...].reshape(toks, -1)
        pre = jnp.dot(latent, lout[c], preferred_element_type=f32)
        pre = pre + jnp.dot(picked, weight, preferred_element_type=f32)
        at = pl.ds(pl.multiple_of(c * blk, blk), blk)
        square = pre * pre
        curve = jnp.tanh(GELU_SCALE * (pre + GELU_CUBIC * (square * pre)))
        half = 0.5 * (1.0 + curve)
        act_ref[:, at] = (pre * half).astype(act_ref.dtype)
        inner = GELU_SCALE * (1.0 + 3.0 * GELU_CUBIC * square)
        deriv = half + 0.5 * pre * (1.0 - curve * curve) * inner
        slope = (cot[:, at].astype(f32) * deriv).astype(jnp.bfloat16)
        grad = lax.dot_general(
            picked, slope, (((0,), (0,)), ((), ())), preferred_element_type=f32)
        own[c] = grad.reshape(per, blk, blk)

    def sum_copy(way, d, j):
        there = z + 1 if way == 0 else z - 1
        return pltpu.make_async_remote_copy(
            src_ref=sbuf.at[d, span(j)], dst_ref=rbuf.at[way, d, span(j)],
            send_sem=rs_send.at[d, j], recv_sem=rs_recv.at[way, d, j],
            device_id={"fsdp": there}, device_id_type=MESH)

    def own_part(d, j):
        return own[span(j), :, pl.ds(pl.multiple_of(d * rows, rows), rows), :]

    def flow(way, d, j, first):
        @pl.when(first)
        def _():
            sbuf[d, span(j)] = own_part(d, j).astype(sbuf.dtype)

        @pl.when(jnp.logical_not(first))
        def _():
            sum_copy(way, d, j).wait_recv()
            sbuf[d, span(j)] = (
                own_part(d, j) + rbuf[way, d, span(j)].astype(f32)).astype(sbuf.dtype)

        sum_copy(way, d, j).start()

    def dp_copy(i, j):
        peer = lax.rem(y + i, ny)
        return pltpu.make_async_remote_copy(
            src_ref=ysend.at[span(j)], dst_ref=yrecv.at[y, span(j)],
            send_sem=y_send.at[i, j], recv_sem=y_recv.at[i, j],
            device_id={"dp": peer}, device_id_type=MESH)

    def step(tau, carry):
        @pl.when(tau + AHEAD < chunks)
        def _():
            send_own(tau + AHEAD)

        def hop(h, carry):
            pass_on(h, tau)
            return carry

        lax.fori_loop(1, nz, hop, 0)

        now = tau - (nz - 2)

        @pl.when(inside(now))
        def _():
            for i in range(nc):
                column(now * nc + i)

        up, down = now - z, now - (nz - 1 - z)

        def towards(d, carry):
            @pl.when(jnp.logical_and(d > z, inside(up)))
            def _():
                flow(0, d, up, z == 0)

            @pl.when(jnp.logical_and(d < z, inside(down)))
            def _():
                flow(1, d, down, z == nz - 1)

            return carry

        lax.fori_loop(0, nz, towards, 0)

        last = now - (nz - 1)

        @pl.when(inside(last))
        def _():
            ysend[span(last)] = own_part(z, last)

            @pl.when(z > 0)
            def _():
                sum_copy(0, z, last).wait_recv()
                ysend[span(last)] += rbuf[0, z, span(last)].astype(f32)

            @pl.when(z < nz - 1)
            def _():
                sum_copy(1, z, last).wait_recv()
                ysend[span(last)] += rbuf[1, z, span(last)].astype(f32)

            for i in range(1, ny):
                dp_copy(i, last).start()
            yrecv[y, span(last)] = ysend[span(last)]

        done = now - nz

        @pl.when(inside(done))
        def _():
            for i in range(1, ny):
                dp_copy(i, done).wait_recv()
            value = yrecv[0, span(done)]
            for i in range(1, ny):
                value = value + yrecv[i, span(done)]
            grad_ref[span(done)] = value

        return carry

    lax.fori_loop(0, chunks + (nz - 2) + nz, step, 0)

    for i in range(1, nt):
        lat_one(i).wait_send()
        lat_two(i, t).wait_send()

    def drain(j, carry):
        for i in range(1, ny):
            dp_copy(i, j).wait_send()

        def each(s, carry):
            @pl.when(jnp.logical_and(s <= z, z < nz - 1))
            def _():
                gather_copy(0, s, j, False).wait_send()

            @pl.when(jnp.logical_and(s >= z, z > 0))
            def _():
                gather_copy(1, s, j, False).wait_send()

            @pl.when(s > z)
            def _():
                sum_copy(0, s, j).wait_send()

            @pl.when(s < z)
            def _():
                sum_copy(1, s, j).wait_send()

            return carry

        return lax.fori_loop(0, nz, each, carry)

    lax.fori_loop(0, chunks, drain, 0)


def on_device(sizes, tokens, panels, block_rows, low_in, low_out, cotangent):
    nz, ny, nt = sizes
    cols, per, rows, blk = panels.shape
    toks, rank = tokens.shape[0], low_in.shape[1]
    nc = 2 if cols % 2 == 0 else 1
    chunks = cols // nc
    bf16, f32 = jnp.bfloat16, jnp.float32
    hop_type = bf16 if nz <= 4 else f32
    low_out = low_out.reshape(cols, rank, blk)
    hbm = pl.BlockSpec(memory_space=pl.ANY)
    vmem = pl.BlockSpec(memory_space=pltpu.VMEM)
    dma = pltpu.SemaphoreType.DMA
    return pl.pallas_call(
        functools.partial(kernel, nz, ny, nt, nc),
        out_shape=(
            jax.ShapeDtypeStruct(cotangent.shape, bf16),
            jax.ShapeDtypeStruct(panels.shape, f32),
        ),
        in_specs=[hbm, hbm, pl.BlockSpec(memory_space=pltpu.SMEM), hbm, hbm, hbm],
        out_specs=(vmem, vmem),
        scratch_shapes=[
            pltpu.VMEM((tokens.shape[1] // blk, toks, blk), bf16),
            pltpu.VMEM(low_in.shape, bf16),
            pltpu.VMEM(low_out.shape, bf16),
            pltpu.VMEM(cotangent.shape, bf16),
            pltpu.VMEM((nz,) + panels.shape, bf16),
            pltpu.VMEM((cols, per, blk, blk), f32),
            pltpu.VMEM((nz,) + panels.shape, hop_type),
            pltpu.VMEM((2, nz) + panels.shape, hop_type),
            pltpu.VMEM(panels.shape, f32),
            pltpu.VMEM((ny,) + panels.shape, f32),
            pltpu.VMEM((nt, toks // nt, rank), f32),
            pltpu.VMEM((nt, toks // nt, rank), f32),
            pltpu.VMEM((nt, toks // nt, rank), bf16),
            dma((4,)),
            dma((tokens.shape[1] // blk,)),
            dma((2, nz, chunks)),
            dma((nz, chunks)),
            dma((nz, chunks)),
            dma((2, nz, chunks)),
            dma((ny, chunks)),
            dma((ny, chunks)),
            dma((nt,)),
            dma((nt,)),
            dma((nt,)),
            dma((nt,)),
        ],
        compiler_params=pltpu.CompilerParams(
            collective_id=0, has_side_effects=True, vmem_limit_bytes=60 * 1024 * 1024),
    )(tokens, panels, block_rows, low_in, low_out, cotangent)


def solution(mesh):
    in_specs = (
        P(("fsdp", "dp"), None),
        P("tensor", None, "fsdp", None),
        P("tensor", None),
        P("tensor", None),
        P("tensor", None, None, None),
        P(("fsdp", "dp"), "tensor"),
    )
    out_specs = (P(("fsdp", "dp"), "tensor"), P("tensor", None, "fsdp", None))
    sizes = tuple(mesh.shape[name] for name in ("fsdp", "dp", "tensor"))
    return jax.shard_map(
        functools.partial(on_device, sizes),
        mesh=mesh, in_specs=in_specs, out_specs=out_specs, check_vma=False,
    )
```

```python
import functools
import math

import jax
import jax.numpy as jnp
from jax import lax
from jax.experimental import pallas as pl
from jax.experimental.pallas import tpu as pltpu
from jax.sharding import PartitionSpec as P

MESH = pl.DeviceIdType.MESH
GELU_SCALE = math.sqrt(2.0 / math.pi)
GELU_CUBIC = 0.044715
AHEAD = 2
SPLIT = (1, 1)
EARLY = (1, 2)


def chosen(pattern, j):
    count, period = pattern
    return lax.rem(j * count, period) < count


def either(pattern, j, act):
    if pattern[0] == pattern[1]:
        act(True)
    elif pattern[0] == 0:
        act(False)
    else:
        pl.when(chosen(pattern, j))(lambda: act(True))
        pl.when(jnp.logical_not(chosen(pattern, j)))(lambda: act(False))


def kernel(
    nz, ny, nt, per,
    tokens_hbm, panels_hbm, rows_hbm, low_in_hbm, low_out_hbm, cot_hbm,
    act_ref, grad_ref,
    rows_ref, tok, lin, lout, cot, pan, own, sbuf, rbuf, ysend, yrecv, xsend, xrecv,
    lpart, lrecv, lat,
    local_sem, tok_sem, ag_send, ag_recv, ay_send, ay_recv, rs_send, rs_recv,
    y_send, y_recv, x_send, x_recv, l1_send, l1_recv, l2_send, l2_recv,
):
    z, y, t = lax.axis_index("fsdp"), lax.axis_index("dp"), lax.axis_index("tensor")
    cells, rows, blk = panels_hbm.shape
    chunks = ag_recv.shape[1]
    size = cells // chunks
    part = size // ny
    nc = size // per
    f32 = jnp.float32

    in_copies = [
        pltpu.make_async_copy(src, dst, local_sem.at[i])
        for i, (src, dst) in enumerate(
            [(low_in_hbm, lin), (panels_hbm, pan.at[z]), (low_out_hbm, lout), (cot_hbm, cot),
             (rows_hbm, rows_ref)]
        )
    ]
    feature_blocks, toks = tok.shape[:2]

    def token_copy(b):
        return pltpu.make_async_copy(
            tokens_hbm.at[:, pl.ds(pl.multiple_of(b * blk, blk), blk)], tok.at[b], tok_sem.at[b])

    def token_start(b, carry):
        token_copy(b).start()
        return carry

    def token_wait(b, carry):
        token_copy(b).wait()
        return carry

    in_copies[0].start()
    lax.fori_loop(0, feature_blocks, token_start, 0)
    for copy in in_copies[1:]:
        copy.start()

    barrier = pltpu.get_barrier_semaphore()

    @pl.when(z > 0)
    def _():
        pl.semaphore_signal(barrier, inc=1, device_id={"fsdp": z - 1}, device_id_type=MESH)

    @pl.when(z < nz - 1)
    def _():
        pl.semaphore_signal(barrier, inc=1, device_id={"fsdp": z + 1}, device_id_type=MESH)

    for i in range(1, nt):
        pl.semaphore_signal(
            barrier, inc=1, device_id={"tensor": lax.rem(t + i, nt)}, device_id_type=MESH)
    for i in range(1, ny):
        pl.semaphore_signal(
            barrier, inc=1, device_id={"dp": lax.rem(y + i, ny)}, device_id_type=MESH)
    neighbours = jnp.where(z > 0, 1, 0) + jnp.where(z < nz - 1, 1, 0)
    pl.semaphore_wait(barrier, nt - 1 + ny - 1 + neighbours)

    def span(j, p=None):
        if p is None:
            return pl.ds(j * size, size)
        return pl.ds(j * size + p * part, part)

    def mine(cut):
        return y if cut else None

    def gather_copy(way, shard, j, cut, from_input=False):
        there = z + 1 if way == 0 else z - 1
        at = span(j, mine(cut))
        src = panels_hbm.at[at] if from_input else pan.at[shard, at]
        return pltpu.make_async_remote_copy(
            src_ref=src, dst_ref=pan.at[shard, at],
            send_sem=ag_send.at[way, shard, j], recv_sem=ag_recv.at[shard, j],
            device_id={"fsdp": there}, device_id_type=MESH)

    def across_copy(i, shard, j, p):
        at = span(j, p)
        return pltpu.make_async_remote_copy(
            src_ref=pan.at[shard, at], dst_ref=pan.at[shard, at],
            send_sem=ay_send.at[i, shard, j], recv_sem=ay_recv.at[i, shard, j],
            device_id={"dp": lax.rem(y + i, ny)}, device_id_type=MESH)

    def send_own(j):
        def act(cut):
            @pl.when(z < nz - 1)
            def _():
                gather_copy(0, z, j, cut, True).start()

            @pl.when(z > 0)
            def _():
                gather_copy(1, z, j, cut, True).start()

        either(SPLIT, j, act)

    def inside(j):
        return jnp.logical_and(j >= 0, j < chunks)

    def pass_on(h, tau):
        j = tau - (h - 1)
        ok = inside(j)

        def arrived(way, shard, more):
            def act(cut):
                gather_copy(way, shard, j, cut).wait_recv()

                @pl.when(more)
                def _():
                    gather_copy(way, shard, j, cut).start()

                if cut:
                    for i in range(1, ny):
                        across_copy(i, shard, j, y).start()

            either(SPLIT, j, act)

        @pl.when(jnp.logical_and(ok, z - h >= 0))
        def _():
            arrived(0, z - h, z < nz - 1)

        @pl.when(jnp.logical_and(ok, z + h < nz))
        def _():
            arrived(1, z + h, z > 0)

    for j in range(min(AHEAD, chunks)):
        send_own(jnp.int32(j))

    in_copies[0].wait()
    lax.fori_loop(0, feature_blocks, token_wait, 0)
    blocks = lin.shape[0] // blk
    lpart[...] = jnp.dot(
        jnp.concatenate([tok[t * blocks + b] for b in range(blocks)], axis=1), lin[...],
        preferred_element_type=f32,
    ).reshape(lpart.shape)

    def lat_one(i):
        peer = lax.rem(t + i, nt)
        return pltpu.make_async_remote_copy(
            src_ref=lpart.at[peer], dst_ref=lrecv.at[i],
            send_sem=l1_send.at[i], recv_sem=l1_recv.at[i],
            device_id={"tensor": peer}, device_id_type=MESH)

    def lat_two(i, shard):
        peer = lax.rem(t + i, nt)
        return pltpu.make_async_remote_copy(
            src_ref=lat.at[shard], dst_ref=lat.at[shard],
            send_sem=l2_send.at[i], recv_sem=l2_recv.at[i],
            device_id={"tensor": peer}, device_id_type=MESH)

    for i in range(1, nt):
        lat_one(i).start()

    def latent_sum():
        total = lpart[t]
        for i in range(1, nt):
            lat_one(i).wait_recv()
            total = total + lrecv[i]
        lat[t] = total.astype(lat.dtype)
        for i in range(1, nt):
            lat_two(i, t).start()
        for copy in in_copies[1:]:
            copy.wait()

    def latent_done():
        for i in range(1, nt):
            lat_two(i, lax.rem(t + nt - i, nt)).wait_recv()

    def column(c):
        picked = jnp.concatenate([tok[rows_ref[c, k]] for k in range(per)], axis=1)
        weight = jnp.concatenate(
            [pan[s, c * per + k] for k in range(per) for s in range(nz)], axis=0)
        latent = lat[...].reshape(toks, -1)
        pre = jnp.dot(latent, lout[c], preferred_element_type=f32)
        pre = pre + jnp.dot(picked, weight, preferred_element_type=f32)
        at = pl.ds(pl.multiple_of(c * blk, blk), blk)
        square = pre * pre
        curve = jnp.tanh(GELU_SCALE * (pre + GELU_CUBIC * (square * pre)))
        half = 0.5 * (1.0 + curve)
        act_ref[:, at] = (pre * half).astype(act_ref.dtype)
        inner = GELU_SCALE * (1.0 + 3.0 * GELU_CUBIC * square)
        deriv = half + 0.5 * pre * (1.0 - curve * curve) * inner
        slope = (cot[:, at].astype(f32) * deriv).astype(jnp.bfloat16)
        grad = lax.dot_general(
            picked, slope, (((0,), (0,)), ((), ())), preferred_element_type=f32)
        own[pl.ds(c * per, per)] = grad.reshape(per, blk, blk)

    def sum_copy(way, d, j, cut):
        there = z + 1 if way == 0 else z - 1
        at = span(j, mine(cut))
        return pltpu.make_async_remote_copy(
            src_ref=sbuf.at[d, at], dst_ref=rbuf.at[way, d, at],
            send_sem=rs_send.at[d, j], recv_sem=rs_recv.at[way, d, j],
            device_id={"fsdp": there}, device_id_type=MESH)

    def own_part(d, at):
        return own[at, pl.ds(pl.multiple_of(d * rows, rows), rows), :]

    def flow(way, d, j, first):
        def act(cut):
            at = span(j, mine(cut))

            @pl.when(first)
            def _():
                sbuf[d, at] = own_part(d, at).astype(sbuf.dtype)

            @pl.when(jnp.logical_not(first))
            def _():
                sum_copy(way, d, j, cut).wait_recv()
                sbuf[d, at] = (own_part(d, at) + rbuf[way, d, at].astype(f32)).astype(sbuf.dtype)

            sum_copy(way, d, j, cut).start()

        either(EARLY, j, act)

    def early_copy(i, j):
        peer = lax.rem(y + i, ny)
        return pltpu.make_async_remote_copy(
            src_ref=xsend.at[span(j, peer)], dst_ref=xrecv.at[y, pl.ds(j * part, part)],
            send_sem=x_send.at[i, j], recv_sem=x_recv.at[i, j],
            device_id={"dp": peer}, device_id_type=MESH)

    def early_start(j):
        def act(cut):
            if cut:
                for i in range(1, ny):
                    at = span(j, lax.rem(y + i, ny))
                    xsend[at] = own[at].astype(xsend.dtype)
                    early_copy(i, j).start()

        either(EARLY, j, act)

    def early_done(j):
        def act(cut):
            if cut:
                total = own[span(j, y)]
                for i in range(1, ny):
                    early_copy(i, j).wait_recv()
                    total = total + xrecv[lax.rem(y + i, ny), pl.ds(j * part, part)].astype(f32)
                own[span(j, y)] = total

        either(EARLY, j, act)

    def dp_copy(i, j, cut):
        at = span(j, mine(cut))
        return pltpu.make_async_remote_copy(
            src_ref=ysend.at[at], dst_ref=yrecv.at[y, at],
            send_sem=y_send.at[i, j], recv_sem=y_recv.at[i, j],
            device_id={"dp": lax.rem(y + i, ny)}, device_id_type=MESH)

    def finish(j):
        def act(cut):
            at = span(j, mine(cut))

            def landed(way):
                sum_copy(way, z, j, cut).wait_recv()
                return rbuf[way, z, at].astype(f32)

            @pl.when(z == 0)
            def _():
                ysend[at] = (own_part(z, at) + landed(1)).astype(ysend.dtype)

            @pl.when(z == nz - 1)
            def _():
                ysend[at] = (own_part(z, at) + landed(0)).astype(ysend.dtype)

            @pl.when(jnp.logical_and(z > 0, z < nz - 1))
            def _():
                ysend[at] = (own_part(z, at) + landed(0) + landed(1)).astype(ysend.dtype)

            for i in range(1, ny):
                dp_copy(i, j, cut).start()
            yrecv[y, at] = ysend[at]

        either(EARLY, j, act)

    def result(j):
        def act(cut):
            for i in range(1, ny):
                dp_copy(i, j, cut).wait_recv()
            if cut:
                for p in range(ny):
                    grad_ref[span(j, p)] = yrecv[p, span(j, p)].astype(f32)
            else:
                value = yrecv[0, span(j)].astype(f32)
                for p in range(1, ny):
                    value = value + yrecv[p, span(j)].astype(f32)
                grad_ref[span(j)] = value

        either(EARLY, j, act)

    def across_done(j):
        def act(cut):
            if cut:
                for i in range(1, ny):
                    def each(s, carry):
                        @pl.when(s != z)
                        def _():
                            across_copy(i, s, j, lax.rem(y + ny - i, ny)).wait_recv()

                        return carry

                    lax.fori_loop(0, nz, each, 0)

        either(SPLIT, j, act)

    def step(tau, carry):
        @pl.when(tau + AHEAD < chunks)
        def _():
            send_own(tau + AHEAD)

        def hop(h, carry):
            pass_on(h, tau)
            return carry

        lax.fori_loop(1, nz, hop, 0)

        pl.when(tau == 0)(latent_sum)
        pl.when(tau == 1)(latent_done)
        now = tau - (nz - 1)

        @pl.when(inside(now))
        def _():
            across_done(now)
            for i in range(nc):
                column(now * nc + i)
            early_start(now)

        summed = now - 1 if EARLY[0] else now
        if EARLY[0]:
            pl.when(inside(summed))(lambda: early_done(summed))
        up, down = summed - z, summed - (nz - 1 - z)

        def towards(d, carry):
            @pl.when(jnp.logical_and(d > z, inside(up)))
            def _():
                flow(0, d, up, z == 0)

            @pl.when(jnp.logical_and(d < z, inside(down)))
            def _():
                flow(1, d, down, z == nz - 1)

            return carry

        lax.fori_loop(0, nz, towards, 0)
        last = summed - (nz - 1)
        pl.when(inside(last))(lambda: finish(last))
        done = last - 1
        pl.when(inside(done))(lambda: result(done))
        return carry

    lax.fori_loop(0, chunks + 2 * nz - 1 + (1 if EARLY[0] else 0), step, 0)

    for i in range(1, nt):
        lat_one(i).wait_send()
        lat_two(i, t).wait_send()

    def drain(j, carry):
        def panels_left(cut):
            def each(s, carry):
                @pl.when(jnp.logical_and(s <= z, z < nz - 1))
                def _():
                    gather_copy(0, s, j, cut).wait_send()

                @pl.when(jnp.logical_and(s >= z, z > 0))
                def _():
                    gather_copy(1, s, j, cut).wait_send()

                if cut:
                    @pl.when(s != z)
                    def _():
                        for i in range(1, ny):
                            across_copy(i, s, j, y).wait_send()

                return carry

            lax.fori_loop(0, nz, each, 0)

        def sums_left(cut):
            def each(s, carry):
                @pl.when(s > z)
                def _():
                    sum_copy(0, s, j, cut).wait_send()

                @pl.when(s < z)
                def _():
                    sum_copy(1, s, j, cut).wait_send()

                return carry

            lax.fori_loop(0, nz, each, 0)
            for i in range(1, ny):
                dp_copy(i, j, cut).wait_send()
                if cut:
                    early_copy(i, j).wait_send()

        either(SPLIT, j, panels_left)
        either(EARLY, j, sums_left)
        return carry

    lax.fori_loop(0, chunks, drain, 0)


def on_device(sizes, tokens, panels, block_rows, low_in, low_out, cotangent):
    nz, ny, nt = sizes
    cols, per, rows, blk = panels.shape
    toks, rank = tokens.shape[0], low_in.shape[1]
    nc = 4 if cols % 4 == 0 else 2 if cols % 2 == 0 else 1
    chunks = cols // nc
    bf16, f32 = jnp.bfloat16, jnp.float32
    hop_type = bf16 if nz <= 4 and ny <= 2 else f32
    low_out = low_out.reshape(cols, rank, blk)
    cells = panels.reshape(cols * per, rows, blk)
    hbm = pl.BlockSpec(memory_space=pl.ANY)
    vmem = pl.BlockSpec(memory_space=pltpu.VMEM)
    dma = pltpu.SemaphoreType.DMA
    early_cells = cells.shape[0] if EARLY[0] else chunks * ny
    early_tile = (blk, blk) if EARLY[0] else (8, blk)
    activated, grad = pl.pallas_call(
        functools.partial(kernel, nz, ny, nt, per),
        out_shape=(
            jax.ShapeDtypeStruct(cotangent.shape, bf16),
            jax.ShapeDtypeStruct(cells.shape, f32),
        ),
        in_specs=[hbm] * 6,
        out_specs=(vmem, vmem),
        scratch_shapes=[
            pltpu.SMEM(block_rows.shape, jnp.int32),
            pltpu.VMEM((tokens.shape[1] // blk, toks, blk), bf16),
            pltpu.VMEM(low_in.shape, bf16),
            pltpu.VMEM(low_out.shape, bf16),
            pltpu.VMEM(cotangent.shape, bf16),
            pltpu.VMEM((nz,) + cells.shape, bf16),
            pltpu.VMEM((cols * per, blk, blk), f32),
            pltpu.VMEM((nz,) + cells.shape, hop_type),
            pltpu.VMEM((2, nz) + cells.shape, hop_type),
            pltpu.VMEM(cells.shape, hop_type),
            pltpu.VMEM((ny,) + cells.shape, hop_type),
            pltpu.VMEM((early_cells,) + early_tile, hop_type),
            pltpu.VMEM((ny, early_cells // ny) + early_tile, hop_type),
            pltpu.VMEM((nt, toks // nt, rank), f32),
            pltpu.VMEM((nt, toks // nt, rank), f32),
            pltpu.VMEM((nt, toks // nt, rank), bf16),
            dma((5,)),
            dma((tokens.shape[1] // blk,)),
            dma((2, nz, chunks)),
            dma((nz, chunks)),
            dma((ny, nz, chunks)),
            dma((ny, nz, chunks)),
            dma((nz, chunks)),
            dma((2, nz, chunks)),
            dma((ny, chunks)),
            dma((ny, chunks)),
            dma((ny, chunks)),
            dma((ny, chunks)),
            dma((nt,)),
            dma((nt,)),
            dma((nt,)),
            dma((nt,)),
        ],
        compiler_params=pltpu.CompilerParams(
            collective_id=0, has_side_effects=True, vmem_limit_bytes=60 * 1024 * 1024),
    )(tokens, cells, block_rows, low_in, low_out, cotangent)
    return activated, grad.reshape(panels.shape)


def solution(mesh):
    in_specs = (
        P(("fsdp", "dp"), None),
        P("tensor", None, "fsdp", None),
        P("tensor", None),
        P("tensor", None),
        P("tensor", None, None, None),
        P(("fsdp", "dp"), "tensor"),
    )
    out_specs = (P(("fsdp", "dp"), "tensor"), P("tensor", None, "fsdp", None))
    sizes = tuple(mesh.shape[name] for name in ("fsdp", "dp", "tensor"))
    return jax.shard_map(
        functools.partial(on_device, sizes),
        mesh=mesh, in_specs=in_specs, out_specs=out_specs, check_vma=False,
    )
```

```python
import functools
import math

import jax
import jax.numpy as jnp
from jax import lax
from jax.experimental import pallas as pl
from jax.experimental.pallas import tpu as pltpu
from jax.sharding import PartitionSpec as P

MESH = pl.DeviceIdType.MESH
GELU_SCALE = math.sqrt(2.0 / math.pi)
GELU_CUBIC = 0.044715
AHEAD = 2
SPLIT = (1, 1)
EARLY = (1, 2)


def chosen(pattern, j):
    count, period = pattern
    return lax.rem(j * count, period) < count


def either(pattern, j, act):
    if pattern[0] == pattern[1]:
        act(True)
    elif pattern[0] == 0:
        act(False)
    else:
        pl.when(chosen(pattern, j))(lambda: act(True))
        pl.when(jnp.logical_not(chosen(pattern, j)))(lambda: act(False))


def kernel(
    nz, ny, nt, per,
    tokens_hbm, panels_hbm, rows_hbm, low_in_hbm, low_out_hbm, cot_hbm,
    act_ref, grad_ref,
    rows_ref, tok, lin, lout, cot, pan, own, sbuf, rbuf, ysend, yrecv, xsend, xrecv,
    lpart, lrecv, lat,
    local_sem, tok_sem, ag_send, ag_recv, ay_send, ay_recv, rs_send, rs_recv,
    y_send, y_recv, x_send, x_recv, l1_send, l1_recv, l2_send, l2_recv,
):
    z, y, t = lax.axis_index("fsdp"), lax.axis_index("dp"), lax.axis_index("tensor")
    cells, rows, blk = panels_hbm.shape
    chunks = ag_recv.shape[1]
    size = cells // chunks
    part = size // ny
    nc = size // per
    f32 = jnp.float32

    in_copies = [
        pltpu.make_async_copy(src, dst, local_sem.at[i])
        for i, (src, dst) in enumerate(
            [(low_in_hbm, lin), (panels_hbm, pan.at[z]), (low_out_hbm, lout), (cot_hbm, cot),
             (rows_hbm, rows_ref)]
        )
    ]
    feature_blocks, toks = tok.shape[:2]

    def token_copy(b):
        return pltpu.make_async_copy(
            tokens_hbm.at[:, pl.ds(pl.multiple_of(b * blk, blk), blk)], tok.at[b], tok_sem.at[b])

    def token_start(b, carry):
        token_copy(b).start()
        return carry

    def token_wait(b, carry):
        token_copy(b).wait()
        return carry

    in_copies[0].start()
    lax.fori_loop(0, feature_blocks, token_start, 0)
    for copy in in_copies[1:]:
        copy.start()

    barrier = pltpu.get_barrier_semaphore()

    @pl.when(z > 0)
    def _():
        pl.semaphore_signal(barrier, inc=1, device_id={"fsdp": z - 1}, device_id_type=MESH)

    @pl.when(z < nz - 1)
    def _():
        pl.semaphore_signal(barrier, inc=1, device_id={"fsdp": z + 1}, device_id_type=MESH)

    for i in range(1, nt):
        pl.semaphore_signal(
            barrier, inc=1, device_id={"tensor": lax.rem(t + i, nt)}, device_id_type=MESH)
    for i in range(1, ny):
        pl.semaphore_signal(
            barrier, inc=1, device_id={"dp": lax.rem(y + i, ny)}, device_id_type=MESH)
    neighbours = jnp.where(z > 0, 1, 0) + jnp.where(z < nz - 1, 1, 0)
    pl.semaphore_wait(barrier, nt - 1 + ny - 1 + neighbours)

    def span(j, p=None):
        if p is None:
            return pl.ds(j * size, size)
        return pl.ds(j * size + p * part, part)

    def mine(cut):
        return y if cut else None

    def gather_copy(way, shard, j, cut, from_input=False):
        there = z + 1 if way == 0 else z - 1
        at = span(j, mine(cut))
        src = panels_hbm.at[at] if from_input else pan.at[shard, at]
        return pltpu.make_async_remote_copy(
            src_ref=src, dst_ref=pan.at[shard, at],
            send_sem=ag_send.at[way, shard, j], recv_sem=ag_recv.at[shard, j],
            device_id={"fsdp": there}, device_id_type=MESH)

    def across_copy(i, shard, j, p):
        at = span(j, p)
        return pltpu.make_async_remote_copy(
            src_ref=pan.at[shard, at], dst_ref=pan.at[shard, at],
            send_sem=ay_send.at[i, shard, j], recv_sem=ay_recv.at[i, shard, j],
            device_id={"dp": lax.rem(y + i, ny)}, device_id_type=MESH)

    def send_own(j):
        def act(cut):
            @pl.when(z < nz - 1)
            def _():
                gather_copy(0, z, j, cut, True).start()

            @pl.when(z > 0)
            def _():
                gather_copy(1, z, j, cut, True).start()

        either(SPLIT, j, act)

    def inside(j):
        return jnp.logical_and(j >= 0, j < chunks)

    def pass_on(h, tau):
        j = tau - (h - 1)
        ok = inside(j)

        def arrived(way, shard, more):
            def act(cut):
                gather_copy(way, shard, j, cut).wait_recv()

                @pl.when(more)
                def _():
                    gather_copy(way, shard, j, cut).start()

                if cut:
                    for i in range(1, ny):
                        across_copy(i, shard, j, y).start()

            either(SPLIT, j, act)

        @pl.when(jnp.logical_and(ok, z - h >= 0))
        def _():
            arrived(0, z - h, z < nz - 1)

        @pl.when(jnp.logical_and(ok, z + h < nz))
        def _():
            arrived(1, z + h, z > 0)

    for j in range(min(AHEAD, chunks)):
        send_own(jnp.int32(j))

    def lat_one(i):
        peer = lax.rem(t + i, nt)
        return pltpu.make_async_remote_copy(
            src_ref=lpart.at[peer], dst_ref=lrecv.at[i],
            send_sem=l1_send.at[i], recv_sem=l1_recv.at[i],
            device_id={"tensor": peer}, device_id_type=MESH)

    def lat_two(i, shard):
        peer = lax.rem(t + i, nt)
        return pltpu.make_async_remote_copy(
            src_ref=lat.at[shard], dst_ref=lat.at[shard],
            send_sem=l2_send.at[i], recv_sem=l2_recv.at[i],
            device_id={"tensor": peer}, device_id_type=MESH)

    def latent_part():
        in_copies[0].wait()
        lax.fori_loop(0, feature_blocks, token_wait, 0)
        blocks = lin.shape[0] // blk
        lpart[...] = jnp.dot(
            jnp.concatenate([tok[t * blocks + b] for b in range(blocks)], axis=1), lin[...],
            preferred_element_type=f32,
        ).reshape(lpart.shape)
        for i in range(1, nt):
            lat_one(i).start()

    def latent_sum():
        total = lpart[t]
        for i in range(1, nt):
            lat_one(i).wait_recv()
            total = total + lrecv[i]
        lat[t] = total.astype(lat.dtype)
        for i in range(1, nt):
            lat_two(i, t).start()
        for copy in in_copies[1:]:
            copy.wait()

    def latent_done():
        for i in range(1, nt):
            lat_two(i, lax.rem(t + nt - i, nt)).wait_recv()

    def column(c):
        picked = jnp.concatenate([tok[rows_ref[c, k]] for k in range(per)], axis=1)
        weight = jnp.concatenate(
            [pan[s, c * per + k] for k in range(per) for s in range(nz)], axis=0)
        latent = lat[...].reshape(toks, -1)
        pre = jnp.dot(latent, lout[c], preferred_element_type=f32)
        pre = pre + jnp.dot(picked, weight, preferred_element_type=f32)
        at = pl.ds(pl.multiple_of(c * blk, blk), blk)
        square = pre * pre
        curve = jnp.tanh(GELU_SCALE * (pre + GELU_CUBIC * (square * pre)))
        half = 0.5 * (1.0 + curve)
        act_ref[:, at] = (pre * half).astype(act_ref.dtype)
        inner = GELU_SCALE * (1.0 + 3.0 * GELU_CUBIC * square)
        deriv = half + 0.5 * pre * (1.0 - curve * curve) * inner
        slope = (cot[:, at].astype(f32) * deriv).astype(jnp.bfloat16)
        grad = lax.dot_general(
            picked, slope, (((0,), (0,)), ((), ())), preferred_element_type=f32)
        own[pl.ds(c * per, per)] = grad.reshape(per, blk, blk)

    def sum_copy(way, d, j, cut):
        there = z + 1 if way == 0 else z - 1
        at = span(j, mine(cut))
        return pltpu.make_async_remote_copy(
            src_ref=sbuf.at[d, at], dst_ref=rbuf.at[way, d, at],
            send_sem=rs_send.at[d, j], recv_sem=rs_recv.at[way, d, j],
            device_id={"fsdp": there}, device_id_type=MESH)

    def own_part(d, at):
        return own[at, pl.ds(pl.multiple_of(d * rows, rows), rows), :]

    def flow(way, d, j, first):
        def act(cut):
            at = span(j, mine(cut))

            @pl.when(first)
            def _():
                sbuf[d, at] = own_part(d, at).astype(sbuf.dtype)

            @pl.when(jnp.logical_not(first))
            def _():
                sum_copy(way, d, j, cut).wait_recv()
                sbuf[d, at] = (own_part(d, at) + rbuf[way, d, at].astype(f32)).astype(sbuf.dtype)

            sum_copy(way, d, j, cut).start()

        either(EARLY, j, act)

    def early_copy(i, j):
        peer = lax.rem(y + i, ny)
        return pltpu.make_async_remote_copy(
            src_ref=xsend.at[span(j, peer)], dst_ref=xrecv.at[y, pl.ds(j * part, part)],
            send_sem=x_send.at[i, j], recv_sem=x_recv.at[i, j],
            device_id={"dp": peer}, device_id_type=MESH)

    def early_start(j):
        def act(cut):
            if cut:
                for i in range(1, ny):
                    at = span(j, lax.rem(y + i, ny))
                    xsend[at] = own[at].astype(xsend.dtype)
                    early_copy(i, j).start()

        either(EARLY, j, act)

    def early_done(j):
        def act(cut):
            if cut:
                total = own[span(j, y)]
                for i in range(1, ny):
                    early_copy(i, j).wait_recv()
                    total = total + xrecv[lax.rem(y + i, ny), pl.ds(j * part, part)].astype(f32)
                own[span(j, y)] = total

        either(EARLY, j, act)

    def dp_copy(i, j, cut):
        at = span(j, mine(cut))
        return pltpu.make_async_remote_copy(
            src_ref=ysend.at[at], dst_ref=yrecv.at[y, at],
            send_sem=y_send.at[i, j], recv_sem=y_recv.at[i, j],
            device_id={"dp": lax.rem(y + i, ny)}, device_id_type=MESH)

    def finish(j):
        def act(cut):
            at = span(j, mine(cut))

            def landed(way):
                sum_copy(way, z, j, cut).wait_recv()
                return rbuf[way, z, at].astype(f32)

            @pl.when(z == 0)
            def _():
                ysend[at] = (own_part(z, at) + landed(1)).astype(ysend.dtype)

            @pl.when(z == nz - 1)
            def _():
                ysend[at] = (own_part(z, at) + landed(0)).astype(ysend.dtype)

            @pl.when(jnp.logical_and(z > 0, z < nz - 1))
            def _():
                ysend[at] = (own_part(z, at) + landed(0) + landed(1)).astype(ysend.dtype)

            for i in range(1, ny):
                dp_copy(i, j, cut).start()
            yrecv[y, at] = ysend[at]

        either(EARLY, j, act)

    def result(j):
        def act(cut):
            for i in range(1, ny):
                dp_copy(i, j, cut).wait_recv()
            if cut:
                for p in range(ny):
                    grad_ref[span(j, p)] = yrecv[p, span(j, p)].astype(f32)
            else:
                value = yrecv[0, span(j)].astype(f32)
                for p in range(1, ny):
                    value = value + yrecv[p, span(j)].astype(f32)
                grad_ref[span(j)] = value

        either(EARLY, j, act)

    def across_done(j):
        def act(cut):
            if cut:
                for i in range(1, ny):
                    def each(s, carry):
                        @pl.when(s != z)
                        def _():
                            across_copy(i, s, j, lax.rem(y + ny - i, ny)).wait_recv()

                        return carry

                    lax.fori_loop(0, nz, each, 0)

        either(SPLIT, j, act)

    def step(tau, carry):
        @pl.when(tau + AHEAD < chunks)
        def _():
            send_own(tau + AHEAD)

        def hop(h, carry):
            pass_on(h, tau)
            return carry

        lax.fori_loop(1, nz, hop, 0)

        pl.when(tau == 0)(latent_part)
        pl.when(tau == 1)(latent_sum)
        pl.when(tau == 2)(latent_done)
        now = tau - (nz - 1)

        @pl.when(inside(now))
        def _():
            across_done(now)
            for i in range(nc):
                column(now * nc + i)
            early_start(now)

        summed = now - 1 if EARLY[0] else now
        if EARLY[0]:
            pl.when(inside(summed))(lambda: early_done(summed))
        up, down = summed - z, summed - (nz - 1 - z)

        def towards(d, carry):
            far = nz - 1 - d

            @pl.when(jnp.logical_and(far > z, inside(up)))
            def _():
                flow(0, far, up, z == 0)

            @pl.when(jnp.logical_and(d < z, inside(down)))
            def _():
                flow(1, d, down, z == nz - 1)

            return carry

        lax.fori_loop(0, nz, towards, 0)
        last = summed - (nz - 1)
        pl.when(inside(last))(lambda: finish(last))
        done = last - 1
        pl.when(inside(done))(lambda: result(done))
        return carry

    lax.fori_loop(0, chunks + 2 * nz - 1 + (1 if EARLY[0] else 0), step, 0)

    for i in range(1, nt):
        lat_one(i).wait_send()
        lat_two(i, t).wait_send()

    def drain(j, carry):
        def panels_left(cut):
            def each(s, carry):
                @pl.when(jnp.logical_and(s <= z, z < nz - 1))
                def _():
                    gather_copy(0, s, j, cut).wait_send()

                @pl.when(jnp.logical_and(s >= z, z > 0))
                def _():
                    gather_copy(1, s, j, cut).wait_send()

                if cut:
                    @pl.when(s != z)
                    def _():
                        for i in range(1, ny):
                            across_copy(i, s, j, y).wait_send()

                return carry

            lax.fori_loop(0, nz, each, 0)

        def sums_left(cut):
            def each(s, carry):
                @pl.when(s > z)
                def _():
                    sum_copy(0, s, j, cut).wait_send()

                @pl.when(s < z)
                def _():
                    sum_copy(1, s, j, cut).wait_send()

                return carry

            lax.fori_loop(0, nz, each, 0)
            for i in range(1, ny):
                dp_copy(i, j, cut).wait_send()
                if cut:
                    early_copy(i, j).wait_send()

        either(SPLIT, j, panels_left)
        either(EARLY, j, sums_left)
        return carry

    lax.fori_loop(0, chunks, drain, 0)


def on_device(sizes, tokens, panels, block_rows, low_in, low_out, cotangent):
    nz, ny, nt = sizes
    cols, per, rows, blk = panels.shape
    toks, rank = tokens.shape[0], low_in.shape[1]
    nc = 4 if cols % 4 == 0 else 2 if cols % 2 == 0 else 1
    chunks = cols // nc
    bf16, f32 = jnp.bfloat16, jnp.float32
    hop_type = bf16 if nz <= 4 and ny <= 2 else f32
    low_out = low_out.reshape(cols, rank, blk)
    cells = panels.reshape(cols * per, rows, blk)
    hbm = pl.BlockSpec(memory_space=pl.ANY)
    vmem = pl.BlockSpec(memory_space=pltpu.VMEM)
    dma = pltpu.SemaphoreType.DMA
    early_cells = cells.shape[0] if EARLY[0] else chunks * ny
    early_tile = (blk, blk) if EARLY[0] else (8, blk)
    activated, grad = pl.pallas_call(
        functools.partial(kernel, nz, ny, nt, per),
        out_shape=(
            jax.ShapeDtypeStruct(cotangent.shape, bf16),
            jax.ShapeDtypeStruct(cells.shape, f32),
        ),
        in_specs=[hbm] * 6,
        out_specs=(vmem, vmem),
        scratch_shapes=[
            pltpu.SMEM(block_rows.shape, jnp.int32),
            pltpu.VMEM((tokens.shape[1] // blk, toks, blk), bf16),
            pltpu.VMEM(low_in.shape, bf16),
            pltpu.VMEM(low_out.shape, bf16),
            pltpu.VMEM(cotangent.shape, bf16),
            pltpu.VMEM((nz,) + cells.shape, bf16),
            pltpu.VMEM((cols * per, blk, blk), f32),
            pltpu.VMEM((nz,) + cells.shape, hop_type),
            pltpu.VMEM((2, nz) + cells.shape, hop_type),
            pltpu.VMEM(cells.shape, hop_type),
            pltpu.VMEM((ny,) + cells.shape, hop_type),
            pltpu.VMEM((early_cells,) + early_tile, hop_type),
            pltpu.VMEM((ny, early_cells // ny) + early_tile, hop_type),
            pltpu.VMEM((nt, toks // nt, rank), f32),
            pltpu.VMEM((nt, toks // nt, rank), f32),
            pltpu.VMEM((nt, toks // nt, rank), bf16),
            dma((5,)),
            dma((tokens.shape[1] // blk,)),
            dma((2, nz, chunks)),
            dma((nz, chunks)),
            dma((ny, nz, chunks)),
            dma((ny, nz, chunks)),
            dma((nz, chunks)),
            dma((2, nz, chunks)),
            dma((ny, chunks)),
            dma((ny, chunks)),
            dma((ny, chunks)),
            dma((ny, chunks)),
            dma((nt,)),
            dma((nt,)),
            dma((nt,)),
            dma((nt,)),
        ],
        compiler_params=pltpu.CompilerParams(
            collective_id=0, has_side_effects=True, vmem_limit_bytes=60 * 1024 * 1024),
    )(tokens, cells, block_rows, low_in, low_out, cotangent)
    return activated, grad.reshape(panels.shape)


def solution(mesh):
    in_specs = (
        P(("fsdp", "dp"), None),
        P("tensor", None, "fsdp", None),
        P("tensor", None),
        P("tensor", None),
        P("tensor", None, None, None),
        P(("fsdp", "dp"), "tensor"),
    )
    out_specs = (P(("fsdp", "dp"), "tensor"), P("tensor", None, "fsdp", None))
    sizes = tuple(mesh.shape[name] for name in ("fsdp", "dp", "tensor"))
    return jax.shard_map(
        functools.partial(on_device, sizes),
        mesh=mesh, in_specs=in_specs, out_specs=out_specs, check_vma=False,
    )
```
